128 devices in a mesh: tok: 16 (over y, z), head: 8 (over x, core).
Axes of the slice: x: 4, y: 4, z: 4, core: 2. Of those that a mesh axis runs over, the one named last changes fastest.
Arguments:
- hidden_in: bfloat16 [16384, 2048], P('tok', 'head'), may hold values from -6 to 6
- qkv_weight: bfloat16 [2048, 6144], P(None, 'head'), may hold values from -0.125 to 0.125
- dense_weight: bfloat16 [2048, 2048], P('head'), may hold values from -0.125 to 0.125
- up_weight: bfloat16 [2048, 8192], P(None, 'head'), may hold values from -0.125 to 0.125
- down_weight: bfloat16 [8192, 2048], P('head'), may hold values from -0.0625 to 0.0625
- attn_gain: float32 [2048], replicated, may hold values from 0.1 to 1.9
- mlp_gain: float32 [2048], replicated, may hold values from 0.1 to 1.9
- suffix_lengths: int32 [16, 4], replicated, may hold values from 1 to 512, 1024 in all within a row
- request_group: int32 [16, 4], replicated, may hold values from 0 to 15
- prefix_slot: int32 [16], replicated, may hold values from 0 to 15, each once
- prefix_cache: bfloat16 [16, 1024, 4096], P('tok', None, 'head'), may hold values from -204 to 204, as said below
Outputs:
- hidden_out: bfloat16 [16384, 2048], P('tok', 'head')
- suffix_cache: bfloat16 [16384, 4096], P('tok', 'head')
The draws below stay inside these ranges and needn't reach their ends.
Inputs may be any that keep to these rules, and one draw needn't show every extreme that they name: `suffix_lengths`: each row sums to 1024, and the largest entry of each row is exactly 512. `prefix_slot`: a permutation of the 16 slots. `prefix_cache`: keys already carry rotary embedding at positions 0 to 1023.
All inputs are finite; a program needn't handle non-finite values.
Results may differ from the reference program's by a relative error of at most 0.015.
Values may be sent and summed in bfloat16 or wider, within the bound.
No kernel may reach another device: no remote copies, remote signals or barrier semaphores. Data moves between devices by JAX's collectives and lax.ppermute only.
A program may use at most 192 MiB of HBM per device.

```python
import math
import jax
import jax.numpy as jnp
import numpy as np
from jax import lax

D = 2048
HEADS = 8
HD = 256
FF = 8192
ROT = 64
TOK_DEV = 1024
REQ_DEV = 4
PREFIX = 1024
MAXLEN = 512
BLOCKS = 16
GROUPS = 16
TOKENS = 16384


def draw_prefix_cache(key, part):
    shape = (GROUPS, PREFIX, HEADS, 2, HD)
    values = jnp.clip(jax.random.normal(key, shape, jnp.float32), -6.0, 6.0)
    return values.reshape(GROUPS, PREFIX, HEADS * 2 * HD).astype(jnp.bfloat16)


def touch_ends(entries, own_key, low, high):
    extent = entries.shape
    place = [jax.random.randint(jax.random.fold_in(own_key, axis), (), 0, extent[axis]) for axis in range(len(extent))]
    entries = entries.at[tuple(place)].set(low)
    longest = extent.index(max(extent))
    place[longest] = (place[longest] + 1) % extent[longest]
    return entries.at[tuple(place)].set(high)


def block_scale(own_key, extent, shards, smallest, top_value):
    factor_of, own = 1.0, jax.random.fold_in(own_key, 6)
    for axis_at, blocks in shards:
        steps = jnp.exp(jax.random.uniform(jax.random.fold_in(own, axis_at), (blocks,), jnp.float32, smallest / len(shards), top_value / len(shards)))
        factor_of = factor_of * jnp.repeat(steps, extent[axis_at] // blocks).reshape([-1 if axis == axis_at else 1 for axis in range(len(extent))])
    return factor_of


def rank_bounds(number_of, slope):
    portions = [(1 << 20) // math.isqrt(rank ** slope) + 1 for rank in range(1, number_of + 1)]
    deviation = 1 + sum(portions) // (1 << 30)
    return np.cumsum(np.array([max(1, weight // deviation) for weight in portions]))


def ranked(key, dims, number_of, lean):
    listing = rank_bounds(number_of, lean)
    lot = jax.random.randint(jax.random.fold_in(key, 1), dims, 0, int(listing[number_of - 1]))
    grade = jnp.searchsorted(jnp.asarray(listing, jnp.int32), lot, side="right")
    return jax.random.permutation(jax.random.fold_in(key, 2), number_of)[grade].astype(jnp.int32)


def length_profile(count, total, bound, lean):
    loads = [(1 << 20) // math.isqrt(standing ** lean) + 1 for standing in range(2, count + 1)]
    rest, holding = total - bound - (count - 1), [1] * (count - 1)
    while rest > 0:
        movable = [i for i in range(count - 1) if holding[i] < bound]
        whole, remaining = sum([loads[i] for i in movable]), rest
        for i in movable:
            extra = min(bound - holding[i], max(1, remaining * loads[i] // whole), rest)
            holding[i] = holding[i] + extra
            rest = rest - extra
    return np.array([bound] + holding)


def uneven_parts(stream_key, number_of, total, limit, skew):
    if number_of == 2:
        one = jax.random.randint(stream_key, (), max(1, total - limit), min(limit, total - 1) + 1)
        return jnp.stack([one, total - one])
    tallies = jnp.asarray(length_profile(number_of, total, limit, skew), jnp.int32)
    couples = (number_of - 1) // 2
    giver, receiver = tallies[1:1 + 2 * couples:2], tallies[2:2 + 2 * couples:2]
    margin = jnp.minimum(giver - 1, limit - receiver)
    passed = jax.random.randint(jax.random.fold_in(stream_key, 1), (couples,), 0, 1 << 20) % (margin + 1)
    tallies = tallies.at[1:1 + 2 * couples:2].set(giver - passed).at[2:2 + 2 * couples:2].set(receiver + passed)
    return tallies[jax.random.permutation(jax.random.fold_in(stream_key, 2), number_of)]


def gaussian(stream_key, shape, scale, limit, pieces=(), kind=jnp.bfloat16):
    values = jax.random.normal(stream_key, shape, jnp.float32) * scale
    if len(pieces) > 0:
        values = block_scale(stream_key, shape, pieces, -0.22, 0.18) * values
    return jnp.clip(values, min=-limit, max=limit).astype(kind)


def setup_inputs(seed: int = 0) -> dict:
    key_of = jax.random.split(jax.random.key(seed), 12)
    return {
        "hidden_in": gaussian(key_of[0], (TOKENS, D), 1.0, 6.0, ((0, 16), (1, 8))),
        "qkv_weight": gaussian(key_of[1], (D, HEADS * 3 * HD), D ** -0.5, 0.125, ((1, 8),)),
        "dense_weight": gaussian(key_of[2], (HEADS * HD, D), (HEADS * HD) ** -0.5, 0.125, ((0, 8),)),
        "up_weight": gaussian(key_of[3], (D, FF), D ** -0.5, 0.125, ((1, 8),)),
        "down_weight": gaussian(key_of[4], (FF, D), FF ** -0.5, 0.0625, ((0, 8),)),
        "attn_gain": jnp.clip(1.0 + 0.18 * jax.random.normal(key_of[5], (D,), jnp.float32), 0.1, 1.9),
        "mlp_gain": jnp.clip(1.0 + 0.18 * jax.random.normal(key_of[6], (D,), jnp.float32), 0.1, 1.9),
        "suffix_lengths": jax.vmap(lambda own: uneven_parts(own, REQ_DEV, TOK_DEV, MAXLEN, 2))(jax.random.split(key_of[7], BLOCKS)).reshape((BLOCKS, REQ_DEV)).astype(jnp.int32),
        "request_group": touch_ends(ranked(key_of[8], (BLOCKS, REQ_DEV), GROUPS, 2), jax.random.fold_in(key_of[8], 3), 0, GROUPS - 1).astype(jnp.int32),
        "prefix_slot": jax.random.permutation(key_of[9], GROUPS).astype(jnp.int32),
        "prefix_cache": draw_prefix_cache(jax.random.fold_in(key_of[11], 71), 0),
    }


def layer_norm(rows, gain):
    values = rows.astype(jnp.float32)
    centre = lax.optimization_barrier(jnp.mean(values, axis=-1, keepdims=True))
    spread = lax.optimization_barrier(jnp.mean(jnp.square(values - centre), axis=-1, keepdims=True))
    return (values - centre) * lax.rsqrt(spread + 1e-05) * gain

def token_layout(lengths, groups, slot_table, count):
    ends = jnp.cumsum(lengths).astype(jnp.int32)
    starts = (ends - lengths).astype(jnp.int32)
    places = jnp.arange(count, dtype=jnp.int32)
    request = lax.optimization_barrier(jnp.sum((places[:, None] >= ends[None, :]).astype(jnp.int32), axis=1)).astype(jnp.int32)
    owned = (request[:, None] == jnp.arange(lengths.shape[0], dtype=jnp.int32)[None, :]).astype(jnp.int32)
    offset = (places - lax.optimization_barrier(jnp.sum(owned * starts[None, :], axis=1))).astype(jnp.int32)
    lookup = (groups[:, None] == jnp.arange(slot_table.shape[0], dtype=jnp.int32)[None, :]).astype(jnp.int32)
    request_slot = lax.optimization_barrier(jnp.sum(lookup * slot_table[None, :], axis=1)).astype(jnp.int32)
    token_slot = lax.optimization_barrier(jnp.sum(owned * request_slot[None, :], axis=1)).astype(jnp.int32)
    return (request, offset, token_slot, request_slot)

def rotate(heads, position, rot_dims):
    halfway = rot_dims // 2
    inverse = 10000.0 ** (-2.0 * jnp.arange(halfway, dtype=jnp.float32) / rot_dims)
    angles = position[:, None] * inverse[None, :]
    cosine = jnp.concatenate([jnp.cos(angles), jnp.cos(angles)], axis=-1)[:, None, :]
    sine_part = jnp.concatenate([jnp.sin(angles), jnp.sin(angles)], axis=-1)[:, None, :]
    turned = heads[..., :rot_dims]
    flipped = jnp.concatenate([-turned[..., halfway:], turned[..., :halfway]], axis=-1)
    return jnp.concatenate([turned * cosine + flipped * sine_part, heads[..., rot_dims:]], axis=-1)

def reference(hidden_in, qkv_weight, dense_weight, up_weight, down_weight, attn_gain, mlp_gain, suffix_lengths, request_group, prefix_slot, prefix_cache):
    scale = HD ** (-0.5)

    def one_block(index):
        rows = lax.dynamic_slice_in_dim(hidden_in, index * TOK_DEV, TOK_DEV, 0)
        request, offset, token_slot, request_slot = token_layout(suffix_lengths[index], request_group[index], prefix_slot, TOK_DEV)
        attn_in = layer_norm(rows, attn_gain).astype(jnp.bfloat16)
        mlp_in = layer_norm(rows, mlp_gain).astype(jnp.bfloat16)
        mixed = jnp.dot(attn_in, qkv_weight, preferred_element_type=jnp.float32).reshape(TOK_DEV, HEADS, 3, HD)
        position = (PREFIX + offset).astype(jnp.float32)
        queries = rotate(mixed[:, :, 0], position, ROT).astype(jnp.bfloat16)
        keys = rotate(mixed[:, :, 1], position, ROT).astype(jnp.bfloat16)
        values = mixed[:, :, 2].astype(jnp.bfloat16)
        cache_rows = jnp.stack([keys, values], axis=2).reshape(TOK_DEV, HEADS * 2 * HD)
        query_f = queries.astype(jnp.float32)
        places = jnp.arange(TOK_DEV, dtype=jnp.int32)
        allowed = (request[:, None] == request[None, :]) & (places[None, :] <= places[:, None])
        own_scores = jnp.einsum('thd,shd->ths', query_f, keys.astype(jnp.float32)) * scale
        own_scores = jnp.where(allowed[:, None, :], own_scores, -1e+30)
        own_top = lax.optimization_barrier(jnp.max(own_scores, axis=-1))
        own_weights = jnp.where(allowed[:, None, :], jnp.exp(own_scores - own_top[..., None]), 0.0)
        own_total = lax.optimization_barrier(jnp.sum(own_weights, axis=-1))
        own_round = lax.optimization_barrier(own_weights.astype(jnp.bfloat16)).astype(jnp.float32)
        own_numer = jnp.einsum('ths,shd->thd', own_round, values.astype(jnp.float32))
        prefix_scores = jnp.zeros((TOK_DEV, HEADS, PREFIX), jnp.float32)
        tables = []
        for which in range(REQ_DEV):
            table = lax.dynamic_index_in_dim(prefix_cache, request_slot[which], 0, keepdims=False).reshape(PREFIX, HEADS, 2, HD).astype(jnp.float32)
            tables.append(table)
            scored = jnp.einsum('thd,phd->thp', query_f, table[:, :, 0]) * scale
            prefix_scores = jnp.where((request == which)[:, None, None], scored, prefix_scores)
        prefix_top = lax.optimization_barrier(jnp.max(prefix_scores, axis=-1))
        prefix_weights = jnp.exp(prefix_scores - prefix_top[..., None])
        prefix_total = lax.optimization_barrier(jnp.sum(prefix_weights, axis=-1))
        prefix_round = lax.optimization_barrier(prefix_weights.astype(jnp.bfloat16)).astype(jnp.float32)
        prefix_numer = jnp.zeros((TOK_DEV, HEADS, HD), jnp.float32)
        for which in range(REQ_DEV):
            added = jnp.einsum('thp,phd->thd', prefix_round, tables[which][:, :, 1])
            prefix_numer = prefix_numer + jnp.where((request == which)[:, None, None], added, 0.0)
        prefix_part = (prefix_numer / prefix_total[..., None]).astype(jnp.bfloat16).astype(jnp.float32)
        top = jnp.maximum(own_top, prefix_top)
        own_factor = jnp.exp(own_top - top)
        far_factor = jnp.exp(prefix_top - top) * prefix_total
        combined = (own_numer * own_factor[..., None] + prefix_part * far_factor[..., None]) / (own_total * own_factor + far_factor)[..., None]
        attended = combined.astype(jnp.bfloat16).reshape(TOK_DEV, HEADS * HD)
        activated = jax.nn.gelu(jnp.dot(mlp_in, up_weight, preferred_element_type=jnp.float32), approximate=False).astype(jnp.bfloat16)
        summed = jnp.dot(attended, dense_weight, preferred_element_type=jnp.float32) + jnp.dot(activated, down_weight, preferred_element_type=jnp.float32)
        result = (rows.astype(jnp.float32) + summed).astype(jnp.bfloat16)
        return (result, cache_rows)
    results, caches = lax.map(one_block, jnp.arange(BLOCKS, dtype=jnp.int32))
    return (results.reshape(TOKENS, D), caches.reshape(TOKENS, HEADS * 2 * HD))
```

```python
import functools

import jax
import jax.numpy as jnp
from jax import lax
from jax.experimental import pallas as pl
from jax.experimental.pallas import tpu as pltpu
from jax.sharding import PartitionSpec as P

HD = 256
ROT = 64
D = 2048
FF_DEV = 1024
TOK = 1024
PREFIX = 1024
NC = 2
R = TOK // NC
TILE = 256
STAT = 16
BOTH = ("tok", "head")
F32 = jnp.float32
BF16 = jnp.bfloat16
NEG = -1e30


def flat(y, z, x, c):
    return ((y * 4 + z) * 4 + x) * 2 + c


def permutation(move):
    return [
        (flat(y, z, x, c), flat(*move(y, z, x, c)))
        for y in range(4)
        for z in range(4)
        for x in range(4)
        for c in range(2)
    ]


def from_x(value, step):
    pairs = permutation(lambda y, z, x, c: (y, z, (x - step) % 4, c))
    return lax.ppermute(value, BOTH, pairs)


def from_core(value):
    return lax.ppermute(value, BOTH, permutation(lambda y, z, x, c: (y, z, x, 1 - c)))


def from_page(value, step):
    return lax.ppermute(
        value,
        BOTH,
        permutation(
            lambda y, z, x, c: (y, (z - step) % 4, x, c) if c == 0 else ((y - step) % 4, z, x, c)
        ),
    )


def from_query(value, step):
    return lax.ppermute(
        value,
        BOTH,
        permutation(
            lambda y, z, x, c: ((y - step) % 4, z, x, c) if c == 0 else (y, (z - step) % 4, x, c)
        ),
    )


def dot(a, b, a_dim, b_dim):
    return lax.dot_general(a, b, (((a_dim,), (b_dim,)), ((), ())), preferred_element_type=F32)


def project_kernel(pos, *refs):
    blocks = refs[:8]
    attn_gain, mlp_gain, weight, cosine, sine, q_ref, kv_ref, mlp_ref, normed = refs[8:]
    rows = q_ref.shape[0]
    step = 64

    def norm(part, carry):
        at = pl.ds(pl.multiple_of(part * step, step), step)
        values = [block[at, :].astype(F32) for block in blocks]
        total = values[0]
        for value in values[1:]:
            total = total + value
        centre = jnp.sum(total, axis=-1, keepdims=True) * (1.0 / D)
        values = [value - centre for value in values]
        square = values[0] * values[0]
        for value in values[1:]:
            square = square + value * value
        spread = jnp.sum(square, axis=-1, keepdims=True) * (1.0 / D)
        inverse = lax.rsqrt(spread + 1e-05)
        for n, value in enumerate(values):
            scaled = value * inverse
            normed[at, n * 256 : (n + 1) * 256] = (scaled * attn_gain[pos[n]]).astype(BF16)
            column = pl.multiple_of(pos[n] * 256, 256)
            mlp_ref[at, pl.ds(column, 256)] = (scaled * mlp_gain[pos[n]]).astype(BF16)
        return carry

    lax.fori_loop(0, rows // step, norm, 0)
    mixed = None
    for n in range(8):
        row = pl.multiple_of(pos[n] * 256, 256)
        part = jnp.dot(
            normed[:, n * 256 : (n + 1) * 256],
            weight[pl.ds(row, 256), :],
            preferred_element_type=F32,
        )
        mixed = part if mixed is None else mixed + part
    lane = lax.broadcasted_iota(jnp.int32, (rows, 128), 1)

    def rotate(head):
        flipped = jnp.where(lane < ROT // 2, pltpu.roll(head, 96, 1), pltpu.roll(head, 32, 1))
        return head * cosine[...] + flipped * sine[...]

    scale = HD ** (-0.5)
    q_ref[:, 0:128] = (rotate(mixed[:, 0:128]) * scale).astype(BF16)
    q_ref[:, 128:256] = (mixed[:, 128:256] * scale).astype(BF16)
    kv_ref[:, 0:128] = rotate(mixed[:, 256:384]).astype(BF16)
    kv_ref[:, 128:512] = mixed[:, 384:768].astype(BF16)


def project(pos, blocks, attn_gain, mlp_gain, weight, cosine, sine):
    rows = blocks[0].shape[0]
    tile = pl.BlockSpec((TILE, 256), lambda i, p: (i, 0))
    gain = pl.BlockSpec((8, 1, 256), lambda i, p: (0, 0, 0))
    table = pl.BlockSpec((TILE, 128), lambda i, p: (i, 0))
    return pl.pallas_call(
        project_kernel,
        grid_spec=pltpu.PrefetchScalarGridSpec(
            num_scalar_prefetch=1,
            grid=(rows // TILE,),
            in_specs=[tile] * 8
            + [gain, gain, pl.BlockSpec((D, 768), lambda i, p: (0, 0)), table, table],
            out_specs=[
                tile,
                pl.BlockSpec((TILE, 512), lambda i, p: (i, 0)),
                pl.BlockSpec((TILE, D), lambda i, p: (i, 0)),
            ],
            scratch_shapes=[pltpu.VMEM((TILE, D), BF16)],
        ),
        out_shape=[
            jax.ShapeDtypeStruct((rows, 256), BF16),
            jax.ShapeDtypeStruct((rows, 512), BF16),
            jax.ShapeDtypeStruct((rows, D), BF16),
        ],
        cost_estimate=pl.CostEstimate(
            flops=2 * rows * D * 768, bytes_accessed=rows * D * 4 + D * 768 * 2, transcendentals=0
        ),
        name="project",
    )(pos, *blocks, attn_gain, mlp_gain, weight, cosine, sine)


def own_kernel(base, q_ref, *refs):
    keys, (first_ref, numer_ref, stat_ref) = refs[:-3], refs[-3:]
    rows = q_ref.shape[0]
    for t in range(rows // TILE):
        q = q_ref[t * TILE : (t + 1) * TILE, :]
        q_at = base + t * TILE
        first = first_ref[:, t * TILE : (t + 1) * TILE]
        spots = range(max(0, q_at - 2 * TILE), q_at + 1, TILE)
        scores = []
        for spot in spots:
            part = keys[spot // R][spot % R : spot % R + TILE, 0:256]
            score = dot(part, q, 1, 1)
            key_at = spot + lax.broadcasted_iota(jnp.int32, (TILE, TILE), 0)
            mine = q_at + lax.broadcasted_iota(jnp.int32, (TILE, TILE), 1)
            scores.append(jnp.where((key_at <= mine) & (key_at >= first), score, NEG))
        top = jnp.max(scores[0], axis=0, keepdims=True)
        for score in scores[1:]:
            top = jnp.maximum(top, jnp.max(score, axis=0, keepdims=True))
        total, numer = None, None
        for spot, score in zip(spots, scores):
            weight = jnp.exp(score - top)
            added = jnp.sum(weight, axis=0, keepdims=True)
            total = added if total is None else total + added
            part = keys[spot // R][spot % R : spot % R + TILE, 256:512]
            out = dot(part, weight.astype(BF16), 0, 0)
            numer = out if numer is None else numer + out
        numer_ref[:, t * TILE : (t + 1) * TILE] = numer
        stat_ref[0:1, t * TILE : (t + 1) * TILE] = top
        stat_ref[1:2, t * TILE : (t + 1) * TILE] = total


def own_attention(base, q, keys, first):
    rows = q.shape[0]
    vmem = pl.BlockSpec(memory_space=pltpu.VMEM)
    return pl.pallas_call(
        functools.partial(own_kernel, base),
        in_specs=[vmem] * (len(keys) + 2),
        out_specs=[vmem, vmem],
        out_shape=[
            jax.ShapeDtypeStruct((256, rows), F32),
            jax.ShapeDtypeStruct((8, rows), F32),
        ],
        cost_estimate=pl.CostEstimate(
            flops=4 * rows * 768 * 256, bytes_accessed=rows * 3072, transcendentals=rows * 768
        ),
        name="own_attention",
    )(q, *keys, first)


def prefix_kernel(base, seg, *refs):
    q_in, page_in, out, (q_buf, page_buf, out_buf, sem) = refs[0:4], refs[4:8], refs[8:12], refs[12:]
    copies = [pltpu.make_async_copy(q_in[k], q_buf.at[k], sem.at[k]) for k in range(4)]
    copies += [pltpu.make_async_copy(page_in[k], page_buf.at[k], sem.at[4 + k]) for k in range(4)]
    for copy in copies:
        copy.start()
    out_buf[...] = jnp.zeros_like(out_buf)
    for copy in copies:
        copy.wait()

    def request(n, carry):
        page = seg[3 * n + 2]
        low = jnp.clip(seg[3 * n] - base, 0, R)
        high = jnp.clip(seg[3 * n + 1] - base, 0, R)
        k = n // 4

        @pl.when((page >= 0) & (high > low))
        def _():
            def visit(t, inner):
                at = pl.multiple_of(t * TILE, TILE)
                score = dot(page_buf[page, :, 0:256], q_buf[k, pl.ds(at, TILE), :], 1, 1)
                top = jnp.max(score, axis=0, keepdims=True)
                weight = jnp.exp(score - top)
                total = jnp.sum(weight, axis=0, keepdims=True)
                numer = dot(page_buf[page, :, 256:512], weight.astype(BF16), 0, 0)
                part = numer * (1.0 / total)
                level = top + jnp.log(total)
                one = level.astype(BF16).astype(F32)
                two = (level - one).astype(BF16).astype(F32)
                three = level - one - two
                row = lax.broadcasted_iota(jnp.int32, (STAT, TILE), 0)
                stat = jnp.where(row == 0, one, jnp.where(row == 1, two, three))
                lane = at + lax.broadcasted_iota(jnp.int32, (1, TILE), 1)
                mine = (lane >= low) & (lane < high)
                old = out_buf[k, 0:256, pl.ds(at, TILE)].astype(F32)
                out_buf[k, 0:256, pl.ds(at, TILE)] = jnp.where(mine, part, old).astype(BF16)
                old = out_buf[k, 256 : 256 + STAT, pl.ds(at, TILE)].astype(F32)
                out_buf[k, 256 : 256 + STAT, pl.ds(at, TILE)] = jnp.where(mine, stat, old).astype(
                    BF16
                )
                return inner

            lax.fori_loop(low // TILE, (high + TILE - 1) // TILE, visit, 0)

        return carry

    lax.fori_loop(0, 16, request, 0)
    backs = [pltpu.make_async_copy(out_buf.at[k], out[k], sem.at[k]) for k in range(4)]
    for copy in backs:
        copy.start()
    for copy in backs:
        copy.wait()


def prefix_attention(base, seg, queries, pages):
    place = pl.BlockSpec(memory_space=pl.ANY)
    return pl.pallas_call(
        functools.partial(prefix_kernel, base),
        grid_spec=pltpu.PrefetchScalarGridSpec(
            num_scalar_prefetch=1,
            grid=(),
            in_specs=[place] * 8,
            out_specs=[place] * 4,
            scratch_shapes=[
                pltpu.VMEM((4, R, 256), BF16),
                pltpu.VMEM((4, PREFIX, 512), BF16),
                pltpu.VMEM((4, 256 + STAT, R), BF16),
                pltpu.SemaphoreType.DMA((8,)),
            ],
        ),
        out_shape=[jax.ShapeDtypeStruct((256 + STAT, R), BF16)] * 4,
        cost_estimate=pl.CostEstimate(
            flops=4 * R * PREFIX * 512, bytes_accessed=6 << 20, transcendentals=R * PREFIX
        ),
        name="prefix_attention",
    )(seg, *queries, *pages)


def join_kernel(block, numer_ref, stat_ref, pick_ref, b0, b1, b2, b3, w_ref, md_ref, att_ref, out_ref):
    @pl.when(pl.program_id(0) == 0)
    def _():
        pick = pick_ref[...]
        part, level = None, None
        for k, back in enumerate((b0, b1, b2, b3)):
            here = back[0:256, :].astype(F32)
            mark = (
                back[256:257, :].astype(F32)
                + back[257:258, :].astype(F32)
                + back[258:259, :].astype(F32)
            )
            part = here if part is None else jnp.where(pick == k, here, part)
            level = mark if level is None else jnp.where(pick == k, mark, level)
        own_top = stat_ref[0:1, :]
        top = jnp.maximum(own_top, level)
        own = jnp.exp(own_top - top)
        far = jnp.exp(level - top)
        under = 1.0 / (stat_ref[1:2, :] * own + far)
        joined = numer_ref[...] * (own * under) + part * (far * under)
        att_ref[...] = jnp.transpose(joined).astype(BF16)

    out = jnp.dot(att_ref[...], w_ref[...], preferred_element_type=F32) + md_ref[...].astype(F32)
    out_ref[0] = out.astype(BF16)


def join(block, numer, stat, pick, backs, weight, md):
    whole = lambda shape: pl.BlockSpec(shape, lambda i, b: (0, 0))
    return pl.pallas_call(
        join_kernel,
        grid_spec=pltpu.PrefetchScalarGridSpec(
            num_scalar_prefetch=1,
            grid=(4,),
            in_specs=[whole((256, R)), whole((8, R)), whole((1, R))]
            + [whole((256 + STAT, R))] * 4
            + [
                pl.BlockSpec((256, 256), lambda i, b: (0, b[i])),
                pl.BlockSpec((R, 256), lambda i, b: (0, b[i])),
            ],
            out_specs=[whole((R, 256)), pl.BlockSpec((1, R, 256), lambda i, b: (i, 0, 0))],
        ),
        out_shape=[
            jax.ShapeDtypeStruct((R, 256), BF16),
            jax.ShapeDtypeStruct((4, R, 256), BF16),
        ],
        cost_estimate=pl.CostEstimate(
            flops=2 * R * 1024 * 256, bytes_accessed=R * 6000, transcendentals=0
        ),
        name="join",
    )(block, numer, stat, pick, *backs, weight, md)


def rest_kernel(block, att_ref, w_ref, md_ref, other_ref, *out):
    for s in range(4):
        at = pl.ds(pl.multiple_of(block[s] * 256, 256), 256)
        value = jnp.dot(att_ref[...], w_ref[:, at], preferred_element_type=F32)
        value = value + md_ref[:, at].astype(F32) + other_ref[s].astype(F32)
        out[s][...] = value.astype(BF16)


def rest(block, att, weight, md, other):
    vmem = pl.BlockSpec(memory_space=pltpu.VMEM)
    return pl.pallas_call(
        rest_kernel,
        grid_spec=pltpu.PrefetchScalarGridSpec(
            num_scalar_prefetch=1, grid=(), in_specs=[vmem] * 4, out_specs=[vmem] * 4
        ),
        out_shape=[jax.ShapeDtypeStruct((R, 256), BF16)] * 4,
        cost_estimate=pl.CostEstimate(
            flops=2 * R * 1024 * 256, bytes_accessed=R * 6000, transcendentals=0
        ),
        name="rest",
    )(block, att, weight, md, other)


def shards(
    hidden_in,
    qkv_weight,
    dense_weight,
    up_weight,
    down_weight,
    attn_gain,
    mlp_gain,
    suffix_lengths,
    request_group,
    prefix_slot,
    prefix_cache,
):
    tok, head = lax.axis_index("tok"), lax.axis_index("head")
    y, z, x, c = tok // 4, tok % 4, head // 2, head % 2
    page_at, query_at = jnp.where(c == 0, z, y), jnp.where(c == 0, y, z)
    steps = jnp.arange(4, dtype=jnp.int32)

    pieces = [hidden_in[n * R : (n + 1) * R] for n in range(NC)]
    near = [[piece] + [from_x(piece, s) for s in (1, 2, 3)] for piece in pieces]
    page = prefix_cache[0]
    pages = [page] + [from_page(page, s) for s in (1, 2, 3)]
    blocks = [group + [from_core(value) for value in group] for group in near]

    ends = jnp.cumsum(suffix_lengths, axis=1)
    starts = ends - suffix_lengths
    hit = request_group[:, :, None] == jnp.arange(16, dtype=jnp.int32)
    slots = jnp.sum(jnp.where(hit, prefix_slot, 0), axis=-1)
    places = jnp.arange(TOK, dtype=jnp.int32)
    my_ends = lax.dynamic_index_in_dim(ends, tok, 0, keepdims=False)
    my_slots = lax.dynamic_index_in_dim(slots, tok, 0, keepdims=False)
    my_starts = lax.dynamic_index_in_dim(starts, tok, 0, keepdims=False)
    request = jnp.sum((places[None, :] >= my_ends[:, None]).astype(jnp.int32), axis=0)
    owned = request[None, :] == steps[:, None]
    first = jnp.sum(jnp.where(owned, my_starts[:, None], 0), axis=0)
    slot = jnp.sum(jnp.where(owned, my_slots[:, None], 0), axis=0)
    pick = (jnp.where(c == 0, slot // 4, slot % 4) - query_at) % 4
    first, pick = first[None, :], pick[None, :]
    position = (PREFIX + places - first[0]).astype(F32)
    inverse = 10000.0 ** (-2.0 * jnp.arange(ROT // 2, dtype=F32) / ROT)
    lane = jnp.arange(128)
    spread = jnp.where(lane < ROT, jnp.tile(inverse, 4), 0.0)
    angle = position[:, None] * spread[None, :]
    cosine = jnp.cos(angle)
    sine = jnp.sin(angle) * jnp.where(lane < ROT // 2, -1.0, 1.0)

    line = (query_at + steps) % 4
    peers = jnp.where(c == 0, line * 4 + z, y * 4 + line)
    peer_slots = slots[peers]
    holder = jnp.where(c == 0, peer_slots // 4, peer_slots % 4)
    held = (jnp.where(c == 0, peer_slots % 4, peer_slots // 4) - page_at) % 4
    held = jnp.where(holder == query_at, held, -1)
    seg = jnp.stack([starts[peers], ends[peers], held], axis=-1).reshape(-1).astype(jnp.int32)

    chips = (x + steps) % 4
    mine, theirs = chips * 2 + c, chips * 2 + 1 - c
    pos = jnp.concatenate([mine, theirs]).astype(jnp.int32)
    gains = [gain.reshape(8, 1, 256) for gain in (attn_gain, mlp_gain)]

    rows = [slice(n * R, (n + 1) * R) for n in range(NC)]
    q, kv, mlp_in = [None] * NC, [None] * NC, [None] * NC
    queries, md, own, backs = [None] * NC, [None] * NC, [None] * NC, [None] * NC
    for n in range(NC):
        q[n], kv[n], mlp_in[n] = project(
            pos, blocks[n], *gains, qkv_weight, cosine[rows[n]], sine[rows[n]]
        )
        queries[n] = [q[n]] + [from_query(q[n], s) for s in (1, 2, 3)]
    for n in range(NC):
        own[n] = own_attention(n * R, q[n], kv[: n + 1], first[:, rows[n]])
        act = jax.nn.gelu(
            jnp.dot(mlp_in[n], up_weight, preferred_element_type=F32), approximate=False
        ).astype(BF16)
        md[n] = jnp.dot(act, down_weight, preferred_element_type=F32).astype(BF16)
    for n in range(NC):
        parts = prefix_attention(n * R, seg, queries[n], pages)
        backs[n] = [parts[0]] + [from_query(parts[(4 - s) % 4], s) for s in (1, 2, 3)]
    done = []
    for n in range(NC):
        att, away = join(
            theirs.astype(jnp.int32), *own[n], pick[:, rows[n]], backs[n], dense_weight, md[n]
        )
        other = from_core(away)
        sums = rest(mine.astype(jnp.int32), att, dense_weight, md[n], other)
        parts = [sums[0]] + [from_x(sums[s], (4 - s) % 4) for s in (1, 2, 3)]
        total = pieces[n].astype(F32)
        for part in parts:
            total = total + part.astype(F32)
        done.append(total.astype(BF16))
    return jnp.concatenate(done, axis=0), jnp.concatenate(kv, axis=0)


def solution(mesh):
    placed = (
        P("tok", "head"),
        P(None, "head"),
        P("head", None),
        P(None, "head"),
        P("head", None),
        P(),
        P(),
        P(),
        P(),
        P(),
        P("tok", None, "head"),
    )
    return jax.shard_map(
        shards,
        mesh=mesh,
        in_specs=placed,
        out_specs=(P("tok", "head"), P("tok", "head")),
        check_vma=False,
    )
```

```python
import functools

import jax
import jax.numpy as jnp
from jax import lax
from jax.experimental import pallas as pl
from jax.experimental.pallas import tpu as pltpu
from jax.sharding import PartitionSpec as P

HD = 256
ROT = 64
D = 2048
FF_DEV = 1024
TOK = 1024
PREFIX = 1024
NC = 2
R = TOK // NC
TILE = 256
STAT = 16
BOTH = ("tok", "head")
F32 = jnp.float32
BF16 = jnp.bfloat16
NEG = -1e30
MIB = 1 << 20
LIMIT_MLP = 18 * MIB
LIMIT_PROJECT = 16 * MIB
LIMIT_OWN = 10 * MIB
LIMIT_PREFIX = 16 * MIB
LIMIT_JOIN = 12 * MIB
LIMIT_REST = 10 * MIB


def flat(y, z, x, c):
    return ((y * 4 + z) * 4 + x) * 2 + c


def permutation(move):
    return [
        (flat(y, z, x, c), flat(*move(y, z, x, c)))
        for y in range(4)
        for z in range(4)
        for x in range(4)
        for c in range(2)
    ]


def permute(value, pairs):
    return lax.ppermute(value, BOTH, pairs)


def from_x(value, step):
    pairs = permutation(lambda y, z, x, c: (y, z, (x - step) % 4, c))
    return permute(value, pairs)


def from_core(value):
    return permute(value, permutation(lambda y, z, x, c: (y, z, x, 1 - c)))


def from_page(value, step):
    return permute(
        value,
        permutation(
            lambda y, z, x, c: (y, (z - step) % 4, x, c) if c == 0 else ((y - step) % 4, z, x, c)
        ),
    )


def from_query(value, step):
    return permute(
        value,
        permutation(
            lambda y, z, x, c: ((y - step) % 4, z, x, c) if c == 0 else (y, (z - step) % 4, x, c)
        ),
    )


def dot(a, b, a_dim, b_dim):
    return lax.dot_general(a, b, (((a_dim,), (b_dim,)), ((), ())), preferred_element_type=F32)


def tie(value, *others):
    return lax.optimization_barrier((value, others))[0]


def kernel_call(body, count, outs, scratch, flops, limit, away=(), tables=1):
    vmem, place = pl.BlockSpec(memory_space=pltpu.VMEM), pl.BlockSpec(memory_space=pltpu.HBM)
    return pl.pallas_call(
        body,
        grid_spec=pltpu.PrefetchScalarGridSpec(
            num_scalar_prefetch=tables,
            grid=(),
            in_specs=[place if n in away else vmem for n in range(count - tables)],
            out_specs=[vmem] * len(outs),
            scratch_shapes=scratch,
        ),
        out_shape=[jax.ShapeDtypeStruct(*out) for out in outs],
        compiler_params=pltpu.CompilerParams(vmem_limit_bytes=limit),
        cost_estimate=pl.CostEstimate(flops=flops, bytes_accessed=4 << 20, transcendentals=0),
    )


def project_kernel(base, pos, *refs):
    blocks = refs[:8]
    attn_gain, mlp_gain, w_hbm, cosine, sine, q_ref, kv_ref, mlp_ref = refs[8:16]
    weight, normed, centre_ref, inverse_ref, sem = refs[16:]
    rows = q_ref.shape[0]
    fetch = pltpu.make_async_copy(w_hbm, weight, sem)
    fetch.start()
    step = 16

    def at_rows(part):
        return pl.ds(pl.multiple_of(part * step, step), step)

    def twice(value):
        return jnp.concatenate([value, value], axis=1)

    def add_up(part, carry):
        at = at_rows(part)
        total = blocks[0][at, :].astype(F32)
        for block in blocks[1:]:
            total = total + block[at, :].astype(F32)
        centre_ref[at, :] = total[:, 0:128] + total[:, 128:256]
        return carry

    def square(part, carry):
        at = at_rows(part)
        centre = twice(centre_ref[at, :])
        total = None
        for block in blocks:
            value = block[at, :].astype(F32) - centre
            total = value * value if total is None else total + value * value
        inverse_ref[at, :] = total[:, 0:128] + total[:, 128:256]
        return carry

    def norm(part, carry):
        at = at_rows(part)
        centre, inverse = twice(centre_ref[at, :]), twice(inverse_ref[at, :])
        for n, block in enumerate(blocks):
            scaled = (block[at, :].astype(F32) - centre) * inverse
            normed[at, n * 256 : (n + 1) * 256] = (scaled * attn_gain[pos[n]]).astype(BF16)
            column = pl.multiple_of(pos[n] * 256, 256)
            mlp_ref[at, pl.ds(column, 256)] = (scaled * mlp_gain[pos[n]]).astype(BF16)
        return carry

    parts = rows // step
    lax.fori_loop(0, parts, add_up, 0, unroll=2)
    centre = jnp.sum(centre_ref[...], axis=-1, keepdims=True) * (1.0 / D)
    centre_ref[...] = jnp.broadcast_to(centre, centre_ref.shape)
    lax.fori_loop(0, parts, square, 0, unroll=2)
    inverse = lax.rsqrt(jnp.sum(inverse_ref[...], axis=-1, keepdims=True) * (1.0 / D) + 1e-05)
    inverse_ref[...] = jnp.broadcast_to(inverse, inverse_ref.shape)
    lax.fori_loop(0, parts, norm, 0, unroll=2)

    fetch.wait()

    def product(kind):
        mixed = None
        for n in range(8):
            row = pl.multiple_of(pos[n] * 256, 256)
            part = jnp.dot(
                normed[:, n * 256 : (n + 1) * 256],
                weight[pl.ds(row, 256), kind * 256 : (kind + 1) * 256],
                preferred_element_type=F32,
            )
            mixed = part if mixed is None else mixed + part
        return mixed

    lane = lax.broadcasted_iota(jnp.int32, (rows, 128), 1)

    def rotate(head):
        flipped = jnp.where(lane < ROT // 2, pltpu.roll(head, 96, 1), pltpu.roll(head, 32, 1))
        return head * cosine[base : base + rows, :] + flipped * sine[base : base + rows, :]

    scale = HD ** (-0.5)
    mixed = product(0)
    q_ref[:, 0:128] = (rotate(mixed[:, 0:128]) * scale).astype(BF16)
    q_ref[:, 128:256] = (mixed[:, 128:256] * scale).astype(BF16)
    mixed = product(1)
    kv_ref[:, 0:128] = rotate(mixed[:, 0:128]).astype(BF16)
    kv_ref[:, 128:256] = mixed[:, 128:256].astype(BF16)
    kv_ref[:, 256:512] = product(2).astype(BF16)


def project(base, pos, blocks, attn_gain, mlp_gain, weight, cosine, sine):
    rows = blocks[0].shape[0]
    return kernel_call(
        functools.partial(project_kernel, base),
        14,
        [((rows, 256), BF16), ((rows, 512), BF16), ((rows, D), BF16)],
        [
            pltpu.VMEM((D, 768), BF16),
            pltpu.VMEM((rows, D), BF16),
            pltpu.VMEM((rows, 128), F32),
            pltpu.VMEM((rows, 128), F32),
            pltpu.SemaphoreType.DMA,
        ],
        2 * rows * D * 768,
        LIMIT_PROJECT,
        away=(10,),
    )(pos, *blocks, attn_gain, mlp_gain, weight, cosine, sine)


def mlp_kernel(block, x_ref, up_ref, down_ref, out_ref, act):
    wide = 512

    def first(n, carry):
        at = pl.ds(pl.multiple_of(n * wide, wide), wide)
        value = jnp.dot(x_ref[...], up_ref[:, at], preferred_element_type=F32)
        value = value * (0.5 + 0.5 * lax.erf(value * (0.5**0.5)))
        act[:, at] = value.astype(BF16)
        return carry

    lax.fori_loop(0, FF_DEV // wide, first, 0)

    def second(n, carry):
        at = pl.ds(pl.multiple_of(block[n] * 256, 256), 256)
        out_ref[n] = jnp.dot(act[...], down_ref[:, at], preferred_element_type=F32).astype(BF16)
        return carry

    lax.fori_loop(0, 8, second, 0)


def mlp(block, x, up, down):
    rows = x.shape[0]
    return kernel_call(
        mlp_kernel,
        4,
        [((8, rows, 256), BF16)],
        [pltpu.VMEM((rows, FF_DEV), BF16)],
        8 * rows * D * 512,
        LIMIT_MLP,
    )(block, x, up, down)[0]


def request_value(starts, values, place):
    found = jnp.full(place.shape, values[0], jnp.int32)
    for j in range(1, 4):
        found = jnp.where(place >= starts[j], values[j], found)
    return found


def own_kernel(base, starts, q_ref, *refs):
    keys, (numer_ref, stat_ref) = refs[:-2], refs[-2:]
    rows = q_ref.shape[0]
    for t in range(rows // TILE):
        q = q_ref[t * TILE : (t + 1) * TILE, :]
        q_at = base + t * TILE
        place = q_at + lax.broadcasted_iota(jnp.int32, (1, TILE), 1)
        first = request_value(starts, [starts[j] for j in range(4)], place)
        spots = range(max(0, q_at - 2 * TILE), q_at + 1, TILE)
        scores = []
        for spot in spots:
            part = keys[spot // R][spot % R : spot % R + TILE, 0:256]
            score = dot(part, q, 1, 1)
            key_at = spot + lax.broadcasted_iota(jnp.int32, (TILE, TILE), 0)
            mine = q_at + lax.broadcasted_iota(jnp.int32, (TILE, TILE), 1)
            scores.append(jnp.where((key_at <= mine) & (key_at >= first), score, NEG))
        top = jnp.max(scores[0], axis=0, keepdims=True)
        for score in scores[1:]:
            top = jnp.maximum(top, jnp.max(score, axis=0, keepdims=True))
        total, numer = None, None
        for spot, score in zip(spots, scores):
            weight = jnp.exp(score - top)
            added = jnp.sum(weight, axis=0, keepdims=True)
            total = added if total is None else total + added
            part = keys[spot // R][spot % R : spot % R + TILE, 256:512]
            out = dot(part, weight.astype(BF16), 0, 0)
            numer = out if numer is None else numer + out
        numer_ref[:, t * TILE : (t + 1) * TILE] = numer
        stat_ref[0:1, t * TILE : (t + 1) * TILE] = top
        stat_ref[1:2, t * TILE : (t + 1) * TILE] = total


def own_attention(base, starts, q, keys):
    rows = q.shape[0]
    return kernel_call(
        functools.partial(own_kernel, base),
        len(keys) + 2,
        [((256, rows), F32), ((8, rows), F32)],
        [],
        4 * rows * 768 * 256,
        LIMIT_OWN,
    )(starts, q, *keys)


def prefix_kernel(base, seg, *refs):
    queries, pages, out = refs[0:4], refs[4:8], refs[8:12]
    q_buf, out_buf, items, counts, sem = refs[12:]
    copies = [pltpu.make_async_copy(queries[k], q_buf.at[k], sem.at[k]) for k in range(4)]
    for copy in copies:
        copy.start()
    for page in range(4):
        counts[page] = 0

    def sort(n, carry):
        page = seg[3 * n + 2]
        low = jnp.clip(seg[3 * n] - base, 0, R)
        high = jnp.clip(seg[3 * n + 1] - base, 0, R)

        @pl.when((page >= 0) & (high > low))
        def _():
            at = page * 16 + counts[page]
            items[at] = n
            counts[page] = counts[page] + 1

        return carry

    lax.fori_loop(0, 16, sort, 0)
    for copy in copies:
        copy.wait()

    for page in range(4):

        def request(spot, carry):
            n = items[page * 16 + spot]
            low = jnp.clip(seg[3 * n] - base, 0, R)
            high = jnp.clip(seg[3 * n + 1] - base, 0, R)
            k = n // 4

            def visit(t, inner):
                at = pl.multiple_of(t * TILE, TILE)
                here = pl.ds(at, TILE)
                score = dot(pages[page][:, 0:256], q_buf[k, here, :], 1, 1)
                top = jnp.max(score, axis=0, keepdims=True)
                weight = jnp.exp(score - top)
                total = jnp.sum(weight, axis=0, keepdims=True)
                numer = dot(pages[page][:, 256:512], weight.astype(BF16), 0, 0)
                part = numer * (1.0 / total)
                level = top + jnp.log(total)
                one = level.astype(BF16).astype(F32)
                two = (level - one).astype(BF16).astype(F32)
                three = level - one - two
                row = lax.broadcasted_iota(jnp.int32, (STAT, TILE), 0)
                stat = jnp.where(row == 0, one, jnp.where(row == 1, two, three))
                lane = at + lax.broadcasted_iota(jnp.int32, (1, TILE), 1)
                mine = (lane >= low) & (lane < high)
                old = out_buf[k, 0:256, here].astype(F32)
                out_buf[k, 0:256, here] = jnp.where(mine, part, old).astype(BF16)
                old = out_buf[k, 256 : 256 + STAT, here].astype(F32)
                out_buf[k, 256 : 256 + STAT, here] = jnp.where(mine, stat, old).astype(BF16)
                return inner

            lax.fori_loop(low // TILE, (high + TILE - 1) // TILE, visit, 0)
            return carry

        lax.fori_loop(0, counts[page], request, 0)
    backs = [pltpu.make_async_copy(out_buf.at[k], out[k], sem.at[k]) for k in range(4)]
    for copy in backs:
        copy.start()
    for copy in backs:
        copy.wait()


def prefix_attention(base, seg, queries, pages):
    return kernel_call(
        functools.partial(prefix_kernel, base),
        9,
        [((256 + STAT, R), BF16)] * 4,
        [
            pltpu.VMEM((4, R, 256), BF16),
            pltpu.VMEM((4, 256 + STAT, R), BF16),
            pltpu.SMEM((64,), jnp.int32),
            pltpu.SMEM((4,), jnp.int32),
            pltpu.SemaphoreType.DMA((4,)),
        ],
        4 * R * PREFIX * 512,
        LIMIT_PREFIX,
    )(seg, *queries, *pages)


def join_kernel(base, block, starts, numer_ref, stat_ref, b0, b1, b2, b3, w_ref, md_ref, att_ref, out_ref):
    place = base + lax.broadcasted_iota(jnp.int32, (1, R), 1)
    pick = request_value(starts, [starts[4 + j] for j in range(4)], place)
    part, level = None, None
    for k, back in enumerate((b0, b1, b2, b3)):
        here = back[0:256, :].astype(F32)
        mark = (
            back[256:257, :].astype(F32)
            + back[257:258, :].astype(F32)
            + back[258:259, :].astype(F32)
        )
        part = here if part is None else jnp.where(pick == k, here, part)
        level = mark if level is None else jnp.where(pick == k, mark, level)
    own_top = stat_ref[0:1, :]
    top = jnp.maximum(own_top, level)
    own = jnp.exp(own_top - top)
    far = jnp.exp(level - top)
    under = 1.0 / (stat_ref[1:2, :] * own + far)
    joined = numer_ref[...] * (own * under) + part * (far * under)
    att_ref[...] = jnp.transpose(joined).astype(BF16)

    def product(s, carry):
        at = pl.ds(pl.multiple_of(block[4 + s] * 256, 256), 256)
        value = jnp.dot(att_ref[...], w_ref[:, at], preferred_element_type=F32)
        out_ref[s] = (value + md_ref[4 + s].astype(F32)).astype(BF16)
        return carry

    lax.fori_loop(0, 4, product, 0)


def join(base, block, starts, numer, stat, backs, weight, md):
    return kernel_call(
        functools.partial(join_kernel, base),
        10,
        [((R, 256), BF16), ((4, R, 256), BF16)],
        [],
        2 * R * 1024 * 256,
        LIMIT_JOIN,
        tables=2,
    )(block, starts, numer, stat, *backs, weight, md)


def rest_kernel(block, att_ref, w_ref, md_ref, other_ref, *out):
    for s in range(4):
        at = pl.ds(pl.multiple_of(block[s] * 256, 256), 256)
        value = jnp.dot(att_ref[...], w_ref[:, at], preferred_element_type=F32)
        value = value + md_ref[s].astype(F32) + other_ref[s].astype(F32)
        out[s][...] = value.astype(BF16)


def rest(block, att, weight, md, other):
    return kernel_call(
        rest_kernel, 5, [((R, 256), BF16)] * 4, [], 2 * R * 1024 * 256, LIMIT_REST
    )(block, att, weight, md, other)


def shards(
    hidden_in,
    qkv_weight,
    dense_weight,
    up_weight,
    down_weight,
    attn_gain,
    mlp_gain,
    suffix_lengths,
    request_group,
    prefix_slot,
    prefix_cache,
):
    tok, head = lax.axis_index("tok"), lax.axis_index("head")
    y, z, x, c = tok // 4, tok % 4, head // 2, head % 2
    page_at, query_at = jnp.where(c == 0, z, y), jnp.where(c == 0, y, z)
    steps = jnp.arange(4, dtype=jnp.int32)

    pieces, near, before = [], [], hidden_in
    for n in range(NC):
        pieces.append(before[n * R : (n + 1) * R])
        near.append([pieces[n]] + [from_x(pieces[n], s) for s in (1, 2, 3)])
        before = tie(hidden_in, *near[-1])
    page = prefix_cache[0]
    pages = [page] + [from_page(page, s) for s in (1, 2, 3)]

    ends = jnp.cumsum(suffix_lengths, axis=1)
    starts = ends - suffix_lengths
    hit = request_group[:, :, None] == jnp.arange(16, dtype=jnp.int32)
    slots = jnp.sum(jnp.where(hit, prefix_slot, 0), axis=-1)
    my_starts = lax.dynamic_index_in_dim(starts, tok, 0, keepdims=False)
    my_slots = lax.dynamic_index_in_dim(slots, tok, 0, keepdims=False)
    my_picks = (jnp.where(c == 0, my_slots // 4, my_slots % 4) - query_at) % 4
    mine_of = jnp.concatenate([my_starts, my_picks]).astype(jnp.int32)
    places = jnp.arange(TOK, dtype=jnp.int32)
    first = request_value(my_starts, my_starts, places)
    position = (PREFIX + places - first).astype(F32)
    inverse = 10000.0 ** (-2.0 * jnp.arange(ROT // 2, dtype=F32) / ROT)
    lane = jnp.arange(128)
    spread = jnp.where(lane < ROT, jnp.tile(inverse, 4), 0.0)
    angle = position[:, None] * spread[None, :]
    cosine = jnp.cos(angle)
    sine = jnp.sin(angle) * jnp.where(lane < ROT // 2, -1.0, 1.0)

    line = (query_at + steps) % 4
    peers = jnp.where(c == 0, line * 4 + z, y * 4 + line)
    chosen = (peers[:, None] == jnp.arange(16, dtype=jnp.int32)).astype(jnp.int32)
    triple = jnp.stack([starts, ends, slots], axis=-1)
    triple = jnp.sum(chosen[:, :, None, None] * triple[None], axis=1)
    peer_slots = triple[:, :, 2]
    holder = jnp.where(c == 0, peer_slots // 4, peer_slots % 4)
    held = (jnp.where(c == 0, peer_slots % 4, peer_slots // 4) - page_at) % 4
    held = jnp.where(holder == query_at, held, -1)
    seg = jnp.concatenate([triple[:, :, 0:2], held[:, :, None]], axis=-1)
    seg = seg.reshape(-1).astype(jnp.int32)

    chips = (x + steps) % 4
    mine, theirs = chips * 2 + c, chips * 2 + 1 - c
    pos = jnp.concatenate([mine, theirs]).astype(jnp.int32)
    gains = [gain.reshape(8, 1, 256) for gain in (attn_gain, mlp_gain)]

    cosine, sine, seg, pos, mine_of = lax.optimization_barrier((cosine, sine, seg, pos, mine_of))
    q, kv, mlp_in = [None] * NC, [None] * NC, [None] * NC
    queries, md, own, backs = [None] * NC, [None] * NC, [None] * NC, [None] * NC
    for n in range(NC):
        group = near[n]
        ready = (cosine, seg) if n == 0 else (q[n - 1],)
        others = [from_core(group[0])] + [from_core(tie(group[s], *ready)) for s in (1, 2, 3)]
        blocks = group + others
        q[n], kv[n], mlp_in[n] = project(
            n * R, pos, blocks, *gains, qkv_weight, cosine, sine
        )
        queries[n] = [q[n]] + [from_query(q[n], s) for s in (1, 2, 3)]
    for n in range(NC):
        own[n] = own_attention(n * R, mine_of, q[n], kv[: n + 1])
    last = own[NC - 1][0]
    done, att, away = [], [None] * NC, [None] * NC
    for n in range(NC):
        queries[n][0] = tie(queries[n][0], last)
        parts = prefix_attention(n * R, seg, queries[n], pages)
        backs[n] = [parts[0]] + [from_query(parts[(4 - s) % 4], s) for s in (1, 2, 3)]
        last = parts[0]
    other, sums = [None] * NC, [None] * NC

    def finish(n):
        sums[n] = rest(pos, att[n], dense_weight, md[n], other[n])
        parts = [sums[n][0]] + [from_x(sums[n][s], (4 - s) % 4) for s in (1, 2, 3)]
        total = pieces[n].astype(F32)
        for part in parts:
            total = total + part.astype(F32)
        done.append(total.astype(BF16))

    for n in range(NC):
        md[n] = mlp(pos, tie(mlp_in[n], last), up_weight, down_weight)
        if n:
            finish(n - 1)
            last = sums[n - 1][0]
        numer, stat = own[n]
        att[n], away[n] = join(
            n * R, pos, mine_of, tie(numer, md[n], last), stat, backs[n], dense_weight, md[n]
        )
        other[n] = from_core(away[n])
        last = away[n]
    finish(NC - 1)
    kv[0] = tie(kv[0], *sums[NC - 1])
    return jnp.concatenate(done, axis=0), jnp.concatenate(kv, axis=0)


def solution(mesh):
    placed = (
        P("tok", "head"),
        P(None, "head"),
        P("head", None),
        P(None, "head"),
        P("head", None),
        P(),
        P(),
        P(),
        P(),
        P(),
        P("tok", None, "head"),
    )
    return jax.shard_map(
        shards,
        mesh=mesh,
        in_specs=placed,
        out_specs=(P("tok", "head"), P("tok", "head")),
        check_vma=False,
    )
```

```python
import functools

import jax
import jax.numpy as jnp
import numpy as np
from jax import lax
from jax.experimental import pallas as pl
from jax.experimental.pallas import tpu as pltpu
from jax.sharding import PartitionSpec as P

HD = 256
ROT = 64
D = 2048
FF_DEV = 1024
TOK = 1024
PREFIX = 1024
NC = 2
R = TOK // NC
TILE = 256
STAT = 16
BOTH = ("tok", "head")
F32 = jnp.float32
BF16 = jnp.bfloat16
NEG = -1e30
MIB = 1 << 20
LIMIT_MLP = 12 * MIB
LIMIT_PROJECT = 12 * MIB
LIMIT_OWN = 6 * MIB
LIMIT_PREFIX = 12 * MIB
LIMIT_JOIN = 6 * MIB
LIMIT_REST = 6 * MIB


def flat(y, z, x, c):
    return ((y * 4 + z) * 4 + x) * 2 + c


def permutation(move):
    return [
        (flat(y, z, x, c), flat(*move(y, z, x, c)))
        for y in range(4)
        for z in range(4)
        for x in range(4)
        for c in range(2)
    ]


def permute(value, pairs):
    return lax.ppermute(value, BOTH, pairs)


def from_x(value, step):
    pairs = permutation(lambda y, z, x, c: (y, z, (x - step) % 4, c))
    return permute(value, pairs)


def from_core(value):
    return permute(value, permutation(lambda y, z, x, c: (y, z, x, 1 - c)))


def from_page(value, step):
    return permute(
        value,
        permutation(
            lambda y, z, x, c: (y, (z - step) % 4, x, c) if c == 0 else ((y - step) % 4, z, x, c)
        ),
    )


def from_query(value, step):
    return permute(
        value,
        permutation(
            lambda y, z, x, c: ((y - step) % 4, z, x, c) if c == 0 else (y, (z - step) % 4, x, c)
        ),
    )


def dot(a, b, a_dim, b_dim):
    return lax.dot_general(a, b, (((a_dim,), (b_dim,)), ((), ())), preferred_element_type=F32)


def tie(value, *others):
    return lax.optimization_barrier((value, others))[0]


def kernel_call(body, count, outs, scratch, flops, limit, away=(), tables=1):
    vmem, place = pl.BlockSpec(memory_space=pltpu.VMEM), pl.BlockSpec(memory_space=pltpu.HBM)
    return pl.pallas_call(
        body,
        grid_spec=pltpu.PrefetchScalarGridSpec(
            num_scalar_prefetch=tables,
            grid=(),
            in_specs=[place if n in away else vmem for n in range(count - tables)],
            out_specs=[vmem] * len(outs),
            scratch_shapes=scratch,
        ),
        out_shape=[jax.ShapeDtypeStruct(*out) for out in outs],
        compiler_params=pltpu.CompilerParams(vmem_limit_bytes=limit),
        cost_estimate=pl.CostEstimate(flops=flops, bytes_accessed=4 << 20, transcendentals=0),
    )


def project_kernel(base, pos, *refs):
    blocks = refs[:8]
    attn_gain, mlp_gain, weight, cosine, sine, q_ref, kv_ref, mlp_ref = refs[8:16]
    normed, centre_ref, inverse_ref = refs[16:]
    rows = q_ref.shape[0]
    step = 16

    def at_rows(part):
        return pl.ds(pl.multiple_of(part * step, step), step)

    def twice(value):
        return jnp.concatenate([value, value], axis=1)

    def add_up(part, carry):
        at = at_rows(part)
        total = blocks[0][at, :].astype(F32)
        for block in blocks[1:]:
            total = total + block[at, :].astype(F32)
        centre_ref[at, :] = total[:, 0:128] + total[:, 128:256]
        return carry

    def square(part, carry):
        at = at_rows(part)
        centre = twice(centre_ref[at, :])
        total = None
        for block in blocks:
            value = block[at, :].astype(F32) - centre
            total = value * value if total is None else total + value * value
        inverse_ref[at, :] = total[:, 0:128] + total[:, 128:256]
        return carry

    def norm(part, carry):
        at = at_rows(part)
        centre, inverse = twice(centre_ref[at, :]), twice(inverse_ref[at, :])
        for n, block in enumerate(blocks):
            scaled = (block[at, :].astype(F32) - centre) * inverse
            normed[at, n * 256 : (n + 1) * 256] = (scaled * attn_gain[pos[n]]).astype(BF16)
            column = pl.multiple_of(pos[n] * 256, 256)
            mlp_ref[at, pl.ds(column, 256)] = (scaled * mlp_gain[pos[n]]).astype(BF16)
        return carry

    parts = rows // step
    lax.fori_loop(0, parts, add_up, 0, unroll=2)
    centre = jnp.sum(centre_ref[...], axis=-1, keepdims=True) * (1.0 / D)
    centre_ref[...] = jnp.broadcast_to(centre, centre_ref.shape)
    lax.fori_loop(0, parts, square, 0, unroll=2)
    inverse = lax.rsqrt(jnp.sum(inverse_ref[...], axis=-1, keepdims=True) * (1.0 / D) + 1e-05)
    inverse_ref[...] = jnp.broadcast_to(inverse, inverse_ref.shape)
    lax.fori_loop(0, parts, norm, 0, unroll=2)

    def product(kind):
        mixed = None
        for n in range(8):
            row = pl.multiple_of(pos[n] * 256, 256)
            part = jnp.dot(
                normed[:, n * 256 : (n + 1) * 256],
                weight[pl.ds(row, 256), kind * 256 : (kind + 1) * 256],
                preferred_element_type=F32,
            )
            mixed = part if mixed is None else mixed + part
        return mixed

    lane = lax.broadcasted_iota(jnp.int32, (rows, 128), 1)

    def rotate(head):
        flipped = jnp.where(lane < ROT // 2, pltpu.roll(head, 96, 1), pltpu.roll(head, 32, 1))
        return head * cosine[base : base + rows, :] + flipped * sine[base : base + rows, :]

    scale = HD ** (-0.5)
    mixed = product(0)
    q_ref[:, 0:128] = (rotate(mixed[:, 0:128]) * scale).astype(BF16)
    q_ref[:, 128:256] = (mixed[:, 128:256] * scale).astype(BF16)
    mixed = product(1)
    kv_ref[:, 0:128] = rotate(mixed[:, 0:128]).astype(BF16)
    kv_ref[:, 128:256] = mixed[:, 128:256].astype(BF16)
    kv_ref[:, 256:512] = product(2).astype(BF16)


def project(base, pos, blocks, attn_gain, mlp_gain, weight, cosine, sine):
    rows = blocks[0].shape[0]
    return kernel_call(
        functools.partial(project_kernel, base),
        14,
        [((rows, 256), BF16), ((rows, 512), BF16), ((rows, D), BF16)],
        [
            pltpu.VMEM((rows, D), BF16),
            pltpu.VMEM((rows, 128), F32),
            pltpu.VMEM((rows, 128), F32),
        ],
        2 * rows * D * 768,
        LIMIT_PROJECT,
    )(pos, *blocks, attn_gain, mlp_gain, weight, cosine, sine)


def mlp_kernel(block, x_ref, up_ref, down_ref, out_ref, act):
    wide = 512

    def first(n, carry):
        at = pl.ds(pl.multiple_of(n * wide, wide), wide)
        value = jnp.dot(x_ref[...], up_ref[:, at], preferred_element_type=F32)
        value = value * (0.5 + 0.5 * lax.erf(value * (0.5**0.5)))
        act[:, at] = value.astype(BF16)
        return carry

    lax.fori_loop(0, FF_DEV // wide, first, 0)

    def second(n, carry):
        at = pl.ds(pl.multiple_of(block[n] * 256, 256), 256)
        out_ref[n] = jnp.dot(act[...], down_ref[:, at], preferred_element_type=F32).astype(BF16)
        return carry

    lax.fori_loop(0, 8, second, 0)


def mlp(block, x, up, down):
    rows = x.shape[0]
    return kernel_call(
        mlp_kernel,
        4,
        [((8, rows, 256), BF16)],
        [pltpu.VMEM((rows, FF_DEV), BF16)],
        8 * rows * D * 512,
        LIMIT_MLP,
    )(block, x, up, down)[0]


def request_value(starts, values, place):
    found = jnp.full(place.shape, values[0], jnp.int32)
    for j in range(1, 4):
        found = jnp.where(place >= starts[j], values[j], found)
    return found


def own_kernel(base, starts, q_ref, *refs):
    keys, (numer_ref, stat_ref) = refs[:-2], refs[-2:]
    rows = q_ref.shape[0]
    for t in range(rows // TILE):
        q = q_ref[t * TILE : (t + 1) * TILE, :]
        q_at = base + t * TILE
        place = q_at + lax.broadcasted_iota(jnp.int32, (1, TILE), 1)
        first = request_value(starts, [starts[j] for j in range(4)], place)
        spots = range(max(0, q_at - 2 * TILE), q_at + 1, TILE)
        scores = []
        for spot in spots:
            part = keys[spot // R][spot % R : spot % R + TILE, 0:256]
            score = dot(part, q, 1, 1)
            key_at = spot + lax.broadcasted_iota(jnp.int32, (TILE, TILE), 0)
            mine = q_at + lax.broadcasted_iota(jnp.int32, (TILE, TILE), 1)
            scores.append(jnp.where((key_at <= mine) & (key_at >= first), score, NEG))
        top = jnp.max(scores[0], axis=0, keepdims=True)
        for score in scores[1:]:
            top = jnp.maximum(top, jnp.max(score, axis=0, keepdims=True))
        total, numer = None, None
        for spot, score in zip(spots, scores):
            weight = jnp.exp(score - top)
            added = jnp.sum(weight, axis=0, keepdims=True)
            total = added if total is None else total + added
            part = keys[spot // R][spot % R : spot % R + TILE, 256:512]
            out = dot(part, weight.astype(BF16), 0, 0)
            numer = out if numer is None else numer + out
        numer_ref[:, t * TILE : (t + 1) * TILE] = numer
        stat_ref[0:1, t * TILE : (t + 1) * TILE] = top
        stat_ref[1:2, t * TILE : (t + 1) * TILE] = total


def own_attention(base, starts, q, keys):
    rows = q.shape[0]
    return kernel_call(
        functools.partial(own_kernel, base),
        len(keys) + 2,
        [((256, rows), F32), ((8, rows), F32)],
        [],
        4 * rows * 768 * 256,
        LIMIT_OWN,
    )(starts, q, *keys)


def prefix_kernel(base, seg, *refs):
    queries, pages, out = refs[0:4], refs[4:8], refs[8:12]
    q_buf, out_buf, items, counts, sem = refs[12:]
    copies = [pltpu.make_async_copy(queries[k], q_buf.at[k], sem.at[k]) for k in range(4)]
    for copy in copies:
        copy.start()
    for page in range(4):
        counts[page] = 0

    def sort(n, carry):
        page = seg[3 * n + 2]
        low = jnp.clip(seg[3 * n] - base, 0, R)
        high = jnp.clip(seg[3 * n + 1] - base, 0, R)

        @pl.when((page >= 0) & (high > low))
        def _():
            at = page * 16 + counts[page]
            items[at] = n
            counts[page] = counts[page] + 1

        return carry

    lax.fori_loop(0, 16, sort, 0)
    for copy in copies:
        copy.wait()

    for page in range(4):

        def request(spot, carry):
            n = items[page * 16 + spot]
            low = jnp.clip(seg[3 * n] - base, 0, R)
            high = jnp.clip(seg[3 * n + 1] - base, 0, R)
            k = n // 4

            begin = jnp.minimum(low // 128 * 128, R - TILE)

            def visit(t, inner):
                at = pl.multiple_of(jnp.minimum(begin + t * TILE, R - TILE), 128)
                here = pl.ds(at, TILE)
                q = q_buf[k, here, :]
                half = PREFIX // 2
                scores = [dot(pages[page][h * half : (h + 1) * half, 0:256], q, 1, 1) for h in range(2)]
                tops = [jnp.max(score, axis=0, keepdims=True) for score in scores]
                weights = [jnp.exp(score - top) for score, top in zip(scores, tops)]
                totals = [jnp.sum(weight, axis=0, keepdims=True) for weight in weights]
                numers = [
                    dot(pages[page][h * half : (h + 1) * half, 256:512], weight.astype(BF16), 0, 0)
                    for h, weight in enumerate(weights)
                ]
                top = jnp.maximum(tops[0], tops[1])
                shares = [jnp.exp(value - top) for value in tops]
                total = totals[0] * shares[0] + totals[1] * shares[1]
                numer = numers[0] * shares[0] + numers[1] * shares[1]
                part = numer * (1.0 / total)
                level = top + jnp.log(total)
                one = level.astype(BF16).astype(F32)
                two = (level - one).astype(BF16).astype(F32)
                three = level - one - two
                row = lax.broadcasted_iota(jnp.int32, (STAT, TILE), 0)
                stat = jnp.where(row == 0, one, jnp.where(row == 1, two, three))
                lane = at + lax.broadcasted_iota(jnp.int32, (1, TILE), 1)
                mine = (lane >= low) & (lane < high)
                old = out_buf[k, 0:256, here].astype(F32)
                out_buf[k, 0:256, here] = jnp.where(mine, part, old).astype(BF16)
                old = out_buf[k, 256 : 256 + STAT, here].astype(F32)
                out_buf[k, 256 : 256 + STAT, here] = jnp.where(mine, stat, old).astype(BF16)
                return inner

            lax.fori_loop(0, (high - begin + TILE - 1) // TILE, visit, 0)
            return carry

        lax.fori_loop(0, counts[page], request, 0)
    backs = [pltpu.make_async_copy(out_buf.at[k], out[k], sem.at[k]) for k in range(4)]
    for copy in backs:
        copy.start()
    for copy in backs:
        copy.wait()


def prefix_attention(base, seg, queries, pages):
    return kernel_call(
        functools.partial(prefix_kernel, base),
        9,
        [((256 + STAT, R), BF16)] * 4,
        [
            pltpu.VMEM((4, R, 256), BF16),
            pltpu.VMEM((4, 256 + STAT, R), BF16),
            pltpu.SMEM((64,), jnp.int32),
            pltpu.SMEM((4,), jnp.int32),
            pltpu.SemaphoreType.DMA((4,)),
        ],
        4 * R * PREFIX * 512,
        LIMIT_PREFIX,
    )(seg, *queries, *pages)


def join_kernel(base, block, starts, numer_ref, stat_ref, b0, b1, b2, b3, w_ref, md_ref, att_ref, out_ref):
    place = base + lax.broadcasted_iota(jnp.int32, (1, R), 1)
    pick = request_value(starts, [starts[4 + j] for j in range(4)], place)
    part, level = None, None
    for k, back in enumerate((b0, b1, b2, b3)):
        here = back[0:256, :].astype(F32)
        mark = (
            back[256:257, :].astype(F32)
            + back[257:258, :].astype(F32)
            + back[258:259, :].astype(F32)
        )
        part = here if part is None else jnp.where(pick == k, here, part)
        level = mark if level is None else jnp.where(pick == k, mark, level)
    own_top = stat_ref[0:1, :]
    top = jnp.maximum(own_top, level)
    own = jnp.exp(own_top - top)
    far = jnp.exp(level - top)
    under = 1.0 / (stat_ref[1:2, :] * own + far)
    joined = numer_ref[...] * (own * under) + part * (far * under)
    att_ref[...] = jnp.transpose(joined).astype(BF16)

    def product(s, carry):
        at = pl.ds(pl.multiple_of(block[4 + s] * 256, 256), 256)
        value = jnp.dot(att_ref[...], w_ref[:, at], preferred_element_type=F32)
        out_ref[s] = (value + md_ref[4 + s].astype(F32)).astype(BF16)
        return carry

    lax.fori_loop(0, 4, product, 0)


def join(base, block, starts, numer, stat, backs, weight, md):
    return kernel_call(
        functools.partial(join_kernel, base),
        10,
        [((R, 256), BF16), ((4, R, 256), BF16)],
        [],
        2 * R * 1024 * 256,
        LIMIT_JOIN,
        tables=2,
    )(block, starts, numer, stat, *backs, weight, md)


def rest_kernel(block, att_ref, w_ref, md_ref, other_ref, *out):
    for s in range(4):
        at = pl.ds(pl.multiple_of(block[s] * 256, 256), 256)
        value = jnp.dot(att_ref[...], w_ref[:, at], preferred_element_type=F32)
        value = value + md_ref[s].astype(F32) + other_ref[s].astype(F32)
        out[s][...] = value.astype(BF16)


def rest(block, att, weight, md, other):
    return kernel_call(
        rest_kernel, 5, [((R, 256), BF16)] * 4, [], 2 * R * 1024 * 256, LIMIT_REST
    )(block, att, weight, md, other)


def shards(
    hidden_in,
    qkv_weight,
    dense_weight,
    up_weight,
    down_weight,
    attn_gain,
    mlp_gain,
    suffix_lengths,
    request_group,
    prefix_slot,
    prefix_cache,
):
    tok, head = lax.axis_index("tok"), lax.axis_index("head")
    y, z, x, c = tok // 4, tok % 4, head // 2, head % 2
    page_at, query_at = jnp.where(c == 0, z, y), jnp.where(c == 0, y, z)
    steps = jnp.arange(4, dtype=jnp.int32)

    pieces, near, before = [], [], hidden_in
    for n in range(NC):
        pieces.append(before[n * R : (n + 1) * R])
        near.append([pieces[n]] + [from_x(pieces[n], s) for s in (1, 2, 3)])
        before = tie(hidden_in, *near[-1])
    page = prefix_cache[0]
    pages = [page] + [from_page(page, s) for s in (1, 2, 3)]

    upto = (steps[None, :] <= steps[:, None]).astype(jnp.int32)
    ends = jnp.sum(suffix_lengths[:, None, :] * upto[None], axis=-1)
    starts = ends - suffix_lengths
    hit = request_group[:, :, None] == jnp.arange(16, dtype=jnp.int32)
    slots = jnp.sum(jnp.where(hit, prefix_slot, 0), axis=-1)
    my_starts = lax.dynamic_index_in_dim(starts, tok, 0, keepdims=False)
    my_slots = lax.dynamic_index_in_dim(slots, tok, 0, keepdims=False)
    my_picks = (jnp.where(c == 0, my_slots // 4, my_slots % 4) - query_at) % 4
    mine_of = jnp.concatenate([my_starts, my_picks]).astype(jnp.int32)
    places = jnp.arange(TOK, dtype=jnp.int32)
    later = jnp.where(places[None, :] >= my_starts[:, None], my_starts[:, None], 0)
    first = jnp.max(later, axis=0)
    position = (PREFIX + places - first).astype(F32)
    lane = jnp.arange(128)
    rates = np.zeros((1, 128), np.float32)
    rates[0, :ROT] = np.tile(10000.0 ** (-2.0 * np.arange(ROT // 2) / ROT), 2)
    angle = position[:, None] * rates
    cosine = jnp.cos(angle)
    sine = jnp.sin(angle) * jnp.where(lane < ROT // 2, -1.0, 1.0)

    line = (query_at + steps) % 4
    peers = jnp.where(c == 0, line * 4 + z, y * 4 + line)
    chosen = (peers[:, None] == jnp.arange(16, dtype=jnp.int32)).astype(jnp.int32)
    triple = jnp.stack([starts, ends, slots], axis=-1)
    triple = jnp.sum(chosen[:, :, None, None] * triple[None], axis=1)
    peer_slots = triple[:, :, 2]
    holder = jnp.where(c == 0, peer_slots // 4, peer_slots % 4)
    held = (jnp.where(c == 0, peer_slots % 4, peer_slots // 4) - page_at) % 4
    held = jnp.where(holder == query_at, held, -1)
    seg = jnp.concatenate([triple[:, :, 0:2], held[:, :, None]], axis=-1)
    seg = seg.reshape(-1).astype(jnp.int32)

    chips = (x + steps) % 4
    mine, theirs = chips * 2 + c, chips * 2 + 1 - c
    pos = jnp.concatenate([mine, theirs]).astype(jnp.int32)
    gains = [gain.reshape(8, 1, 256) for gain in (attn_gain, mlp_gain)]

    cosine, sine, seg, pos, mine_of = lax.optimization_barrier((cosine, sine, seg, pos, mine_of))
    q, kv, mlp_in = [None] * NC, [None] * NC, [None] * NC
    queries, md, own, backs = [None] * NC, [None] * NC, [None] * NC, [None] * NC
    for n in range(NC):
        group = near[n]
        ready = (cosine, seg) if n == 0 else (q[n - 1],)
        others = [from_core(group[0])] + [from_core(tie(group[s], *ready)) for s in (1, 2, 3)]
        blocks = group + others
        q[n], kv[n], mlp_in[n] = project(
            n * R, pos, blocks, *gains, qkv_weight, cosine, sine
        )
        queries[n] = [q[n]] + [from_query(q[n], s) for s in (1, 2, 3)]
    for n in range(NC):
        own[n] = own_attention(n * R, mine_of, q[n], kv[: n + 1])
    last = own[NC - 1][0]
    done, att, away = [], [None] * NC, [None] * NC
    for n in range(NC):
        queries[n][0] = tie(queries[n][0], last)
        parts = prefix_attention(n * R, seg, queries[n], pages)
        backs[n] = [parts[0]] + [from_query(parts[(4 - s) % 4], s) for s in (1, 2, 3)]
        last = parts[0]
    other, sums = [None] * NC, [None] * NC

    def finish(n):
        sums[n] = rest(pos, att[n], dense_weight, md[n], other[n])
        parts = [sums[n][0]] + [from_x(sums[n][s], (4 - s) % 4) for s in (1, 2, 3)]
        total = pieces[n].astype(F32)
        for part in parts:
            total = total + part.astype(F32)
        done.append(total.astype(BF16))

    for n in range(NC):
        md[n] = mlp(pos, tie(mlp_in[n], last), up_weight, down_weight)
        if n:
            finish(n - 1)
            last = sums[n - 1][0]
        numer, stat = own[n]
        att[n], away[n] = join(
            n * R, pos, mine_of, tie(numer, md[n], last), stat, backs[n], dense_weight, md[n]
        )
        other[n] = from_core(away[n])
        last = away[n]
    finish(NC - 1)
    kv[0] = tie(kv[0], *sums[NC - 1])
    return jnp.concatenate(done, axis=0), jnp.concatenate(kv, axis=0)


def solution(mesh):
    placed = (
        P("tok", "head"),
        P(None, "head"),
        P("head", None),
        P(None, "head"),
        P("head", None),
        P(),
        P(),
        P(),
        P(),
        P(),
        P("tok", None, "head"),
    )
    return jax.shard_map(
        shards,
        mesh=mesh,
        in_specs=placed,
        out_specs=(P("tok", "head"), P("tok", "head")),
        check_vma=False,
    )
```
